1024 devices in a mesh: ctx: 16 (over y, x), tp: 64 (over z, core).
Axes of the slice: x: 4, y: 4, z: 32, core: 2. Of those that a mesh axis runs over, the one named last changes fastest.
Arguments:
- short_query: bfloat16 [4096, 32768], P('tp', 'ctx'), may hold values from -16 to 16
- short_key: bfloat16 [4096, 32768], P('tp', 'ctx'), may hold values from -6 to 6
- short_value: bfloat16 [4096, 32768], P('tp', 'ctx'), may hold values from -6 to 6
- short_taps: bfloat16 [4096, 128], P('tp'), may hold values from -0.5 to 0.5
- norm_gain: float32 [4096], P('tp'), may hold values from 0.1 to 1.9
- long_key: bfloat16 [4096, 32768], P('tp', 'ctx'), may hold values from -6 to 6
- long_query: bfloat16 [4096, 32768], P('tp', 'ctx'), may hold values from -6 to 6
- residues: float32 [16, 4096], P(None, 'tp'), may hold values from -1.5 to 1.5
- decay_rates: float32 [16, 4096], P(None, 'tp'), may hold values from 1.5258789e-05 to 0.05
Outputs:
- mixer_output: float32 [4096, 32768], P('tp', 'ctx')
The draws below stay inside these ranges and needn't reach their ends.
All inputs are finite; a program needn't handle non-finite values.
Results may differ from the reference program's by a relative error of at most 0.0029.
Values may be sent and summed in bfloat16 or wider, within the bound.
No kernel may reach another device: no remote copies, remote signals or barrier semaphores. Data moves between devices by JAX's collectives and lax.ppermute only.
A program may use at most 64 MiB of HBM per device.

```python
import math
import jax
import jax.numpy as jnp
from jax import lax

D = 4096
TAPS = 128
MODES = 16
SEQ = 32768


def draw_short_query(key, part):
    value_key = jax.random.fold_in(key, 0)
    channel = jnp.arange(D).astype(jnp.float32)[:, None]
    rising = jnp.sqrt(1.0 + 2.0 * channel / D)
    values = jnp.clip(jax.random.normal(value_key, (D, SEQ), jnp.float32), -4.0, 4.0)
    return (values * rising).astype(jnp.bfloat16)


def block_levels(rng, shape, shards, low, top_value):
    level = 1.0
    for axis_at, blocks in shards:
        steps = jax.random.uniform(jax.random.fold_in(jax.random.fold_in(rng, 6), axis_at), (blocks,), jnp.float32, low / len(shards), top_value / len(shards))
        level = level * jnp.repeat(jnp.exp(steps), shape[axis_at] // blocks).reshape((-1,) + (1,) * (len(shape) - 1 - axis_at))
    return level


def bell_draw(stream_key, extent, deviation, most, shards=(), held_as=jnp.bfloat16):
    gain = block_levels(stream_key, extent, shards, -0.22, 0.18) if shards else 1.0
    entries = jax.random.normal(stream_key, extent, jnp.float32) * deviation * gain
    return jnp.minimum(jnp.maximum(entries, -most), most).astype(held_as)


def setup_inputs(seed: int = 0) -> dict:
    seeds = jax.random.split(jax.random.key(seed), 10)
    return {
        "short_query": draw_short_query(jax.random.fold_in(seeds[9], 71), 0),
        "short_key": bell_draw(seeds[1], (D, SEQ), 1.0, 6.0, ((0, 64), (1, 16))),
        "short_value": bell_draw(seeds[2], (D, SEQ), 1.0, 6.0, ((0, 64), (1, 16))),
        "short_taps": bell_draw(seeds[3], (D, TAPS), TAPS ** -0.5, 0.5, ((0, 64),)),
        "norm_gain": jnp.clip(1.0 + 0.18 * jax.random.normal(seeds[4], (D,), jnp.float32), 0.1, 1.9),
        "long_key": bell_draw(seeds[5], (D, SEQ), 1.0, 6.0, ((0, 64), (1, 16))),
        "long_query": bell_draw(seeds[6], (D, SEQ), 1.0, 6.0, ((0, 64), (1, 16))),
        "residues": bell_draw(seeds[7], (MODES, D), MODES ** -0.5, 1.5, ((1, 64),), jnp.float32),
        "decay_rates": jnp.clip(jnp.exp(math.log(0.05) - 8.094623 * jax.random.uniform(seeds[8], (MODES, D), jnp.float32) ** block_levels(seeds[8], (MODES, D), ((1, 64),), -0.2, 0.2)), 1.52587890625e-05, 0.05),
    }


def make_band(filter_taps):
    tap_count = filter_taps.shape[1]
    row_index = jnp.arange(tap_count)[:, None]
    col_index = jnp.arange(2 * tap_count)[None, :]
    lag_index = row_index + tap_count - col_index
    inside = (lag_index >= 0) & (lag_index < tap_count)
    picked = jnp.take(filter_taps, jnp.clip(lag_index, 0, tap_count - 1), axis=1)
    return jnp.where(inside[None, :, :], picked, jnp.zeros_like(picked))

def short_block(operands):
    extended, filter_taps = operands
    tap_count = filter_taps.shape[1]
    channels, span_len = extended.shape
    length = span_len - tap_count
    block_count = length // tap_count
    earlier = extended[:, :length].reshape(channels, block_count, tap_count)
    current = extended[:, tap_count:].reshape(channels, block_count, tap_count)
    windows = jnp.concatenate([earlier, current], axis=2).astype(jnp.float32)
    band_rows = make_band(filter_taps).astype(jnp.float32)
    mixed = jnp.einsum('cbm,cim->cbi', windows, band_rows, precision=lax.Precision.HIGHEST)
    return mixed.reshape(channels, length)

def long_block(operands):
    signal, residue, decays = operands
    length = signal.shape[1]
    offsets = jnp.arange(length).astype(jnp.float32)
    weights = residue * jnp.sqrt(-jnp.expm1(-2.0 * decays))
    kernel = lax.optimization_barrier(jnp.sum(weights[:, :, None] * jnp.exp(-decays[:, :, None] * offsets[None, None, :]), axis=0))
    spectrum = jnp.fft.rfft(signal, n=2 * length, axis=1) * jnp.fft.rfft(kernel, n=2 * length, axis=1)
    return jnp.fft.irfft(spectrum, n=2 * length, axis=1)[:, :length]

def reference(short_query, short_key, short_value, short_taps, norm_gain, long_key, long_query, residues, decay_rates):
    channels, length = short_value.shape
    tap_count = short_taps.shape[1]
    first_product = (short_key.astype(jnp.float32) * short_value.astype(jnp.float32)).astype(jnp.bfloat16)
    first_product = lax.optimization_barrier(first_product)
    extended = jnp.concatenate([jnp.zeros((channels, tap_count), jnp.bfloat16), first_product], axis=1)
    group_size = min(256, channels)
    group_count = channels // group_size
    short_mix = lax.map(short_block, (extended.reshape(group_count, group_size, length + tap_count), short_taps.reshape(group_count, group_size, tap_count)))
    short_mix = short_mix.reshape(channels, length)
    gated = short_query.astype(jnp.float32) * short_mix
    mean_square = lax.optimization_barrier(jnp.mean(gated * gated, axis=0))
    normed = gated * norm_gain[:, None] * lax.rsqrt(mean_square + 1e-06)[None, :]
    long_input = long_key.astype(jnp.float32) * normed
    mode_count = residues.shape[0]
    lane_count = min(64, channels)
    lane_groups = channels // lane_count
    residue_blocks = residues.reshape(mode_count, lane_groups, lane_count).transpose(1, 0, 2)
    decay_blocks = decay_rates.reshape(mode_count, lane_groups, lane_count).transpose(1, 0, 2)
    long_mix = lax.map(long_block, (long_input.reshape(lane_groups, lane_count, length), residue_blocks, decay_blocks))
    long_mix = long_mix.reshape(channels, length)
    return long_query.astype(jnp.float32) * long_mix
```

```python
import jax
import jax.numpy as jnp
from jax import lax
from jax.experimental import pallas as pl
from jax.experimental.pallas import tpu as pltpu
from jax.sharding import Mesh
from jax.sharding import PartitionSpec as P

D = 4096
TP = ("z", "core")
BLOCK = 128
GROUP = 8
UNROLL = 32
PARTS = 2
INTERPRET = False
f32 = jnp.float32
bf16 = jnp.bfloat16


def call(kernel, out_shape, in_specs, out_specs, scratch=(), flops=0, bytes_accessed=0, limit=40 << 20):
    return pl.pallas_call(
        kernel,
        out_shape=out_shape,
        in_specs=in_specs,
        out_specs=out_specs,
        scratch_shapes=list(scratch),
        compiler_params=pltpu.CompilerParams(vmem_limit_bytes=limit),
        cost_estimate=pl.CostEstimate(
            flops=flops, bytes_accessed=bytes_accessed, transcendentals=0
        ),
        interpret=INTERPRET,
    )


def halves(value):
    high = value.astype(bf16)
    return high, (value - high.astype(f32)).astype(bf16)


def circulant(row):
    spread = jnp.broadcast_to(row, (BLOCK, BLOCK))
    return pltpu.roll(spread, 0, 1, stride=1, stride_axis=0)


def dot(left, right):
    return lax.dot_general(
        left, right, (((1,), (0,)), ((), ())), preferred_element_type=f32
    )


def dot_nt(left, right):
    return lax.dot_general(
        left, right, (((1,), (1,)), ((), ())), preferred_element_type=f32
    )


def upper_mask():
    row = lax.broadcasted_iota(jnp.int32, (BLOCK, BLOCK), 0)
    lane = lax.broadcasted_iota(jnp.int32, (BLOCK, BLOCK), 1)
    return lane >= row


def own_lanes():
    row = lax.broadcasted_iota(jnp.int32, (GROUP, BLOCK), 0)
    lane = lax.broadcasted_iota(jnp.int32, (GROUP, BLOCK), 1)
    return lane % GROUP == row


def short_kernel(
    taps_hbm, key_hbm, value_hbm, mixed_ref, last_ref,
    taps_ref, key_ref, value_ref, taps, xs, ps, sems,
):
    channels, length = key_ref.shape
    blocks = length // BLOCK
    part = channels // PARTS
    first = pltpu.make_async_copy(taps_hbm, taps_ref, sems.at[2 * PARTS])
    first.start()
    copies = []
    for i in range(PARTS):
        rows = pl.ds(i * part, part)
        pair = [
            pltpu.make_async_copy(source.at[rows], target.at[rows], sems.at[2 * i + k])
            for k, (source, target) in enumerate(
                ((key_hbm, key_ref), (value_hbm, value_ref))
            )
        ]
        for copy in pair:
            copy.start()
        copies.append(pair)
    upper = upper_mask()

    def one(c, carry):
        ring = circulant(taps[pl.ds(c, 1), :])
        zero = jnp.zeros_like(ring)
        band = jnp.concatenate(
            [jnp.where(upper, ring, zero), jnp.where(upper, zero, ring)], axis=1
        ).astype(bf16)
        both = dot(xs[pl.ds(c, blocks, stride=channels), :].astype(bf16), band)
        mixed_ref[pl.ds(c, blocks, stride=channels), :] = both[:, :BLOCK]
        ps[pl.ds(c + channels, blocks, stride=channels), :] = both[:, BLOCK:]
        return carry

    first.wait()
    taps[...] = taps_ref[...].astype(f32)
    for i in range(PARTS):
        for copy in copies[i]:
            copy.wait()
        own = slice(i * part, (i + 1) * part)
        for b in range(blocks):
            cols = slice(b * BLOCK, (b + 1) * BLOCK)
            at = b * channels + i * part
            xs[at : at + part, :] = key_ref[own, cols].astype(f32) * value_ref[
                own, cols
            ].astype(f32)
        lax.fori_loop(i * part, (i + 1) * part, one, 0, unroll=UNROLL)
    last_ref[...] = ps[blocks * channels :, :]
    mixed_ref[channels:, :] += ps[channels : blocks * channels, :]


def gate_kernel(
    taps_ref, gain_ref, query_hbm, key_hbm,
    mixed_ref, squares_ref, open_mix, open_query, open_key, query_ref, key_ref, sems,
):
    copies = [
        pltpu.make_async_copy(query_hbm, query_ref, sems.at[0]),
        pltpu.make_async_copy(key_hbm, key_ref, sems.at[1]),
    ]
    for copy in copies:
        copy.start()
    channels, length = query_ref.shape
    blocks = length // BLOCK
    row = lax.broadcasted_iota(jnp.int32, (channels, channels), 0)
    lane = lax.broadcasted_iota(jnp.int32, (channels, channels), 1)
    spread = jnp.broadcast_to(gain_ref[...], (channels, channels))
    gain = jnp.sum(jnp.where(row == lane, spread, 0.0), axis=1, keepdims=True)
    for copy in copies:
        copy.wait()
    open_query[...] = query_ref[:, :BLOCK].astype(f32)
    open_key[...] = gain * key_ref[:, :BLOCK].astype(f32)
    open_mix[...] = taps_ref[:channels, :]
    mixed_ref[:channels, :] = jnp.zeros((channels, BLOCK), f32)
    squares_ref[0:1, :] = jnp.zeros((1, BLOCK), f32)
    for b in range(1, blocks):
        cols = slice(b * BLOCK, (b + 1) * BLOCK)
        rows = slice(b * channels, (b + 1) * channels)
        gated = query_ref[:, cols].astype(f32) * taps_ref[rows, :]
        squares_ref[b : b + 1, :] = jnp.sum(gated * gated, axis=0, keepdims=True)
        mixed_ref[rows, :] = gated * gain * key_ref[:, cols].astype(f32)


def table_kernel(decay_ref, weight_ref, into_hi, into_lo, out_hi, out_lo, long_taps_ref):
    groups = decay_ref.shape[1]
    lane = lax.broadcasted_iota(jnp.int32, (1, BLOCK), 1).astype(f32)
    for g in range(groups):
        rows = slice(g * BLOCK, (g + 1) * BLOCK)
        decay = decay_ref[:, g : g + 1]
        weight = weight_ref[:, g : g + 1]
        into_hi[rows, :], into_lo[rows, :] = halves(jnp.exp(-decay * (BLOCK - lane)))
        out = weight * jnp.exp(-decay * lane)
        out_hi[rows, :], out_lo[rows, :] = halves(out)
        long_taps_ref[g * GROUP : (g + 1) * GROUP, :] = jnp.sum(
            out.reshape(BLOCK // GROUP, GROUP, BLOCK), axis=0
        )


def join_kernel(short_ref, halo_ref, query_ref, key_ref, rest_ref, mixed_ref, squares_ref):
    gated = query_ref[...] * (short_ref[...] + halo_ref[...])
    squares_ref[...] = rest_ref[...]
    squares_ref[0:1, :] = jnp.sum(gated * gated, axis=0, keepdims=True)
    mixed_ref[...] = gated * key_ref[...]


def state_kernel(
    first_ref, mixed_ref, squares_ref, into_hi, into_lo, decay_ref,
    signal_ref, states_ref, last_ref,
):
    groups = decay_ref.shape[0]
    channels = groups * GROUP
    blocks = mixed_ref.shape[0] // channels
    own = own_lanes()
    scales = lax.rsqrt(squares_ref[...] / D + 1e-06)
    signal_ref[:channels, :] = first_ref[...] * scales[0:1, :]
    for b in range(1, blocks):
        rows = slice(b * channels, (b + 1) * channels)
        signal_ref[rows, :] = mixed_ref[rows, :] * scales[b : b + 1, :]
    for g in range(groups):
        rows = slice(g * BLOCK, (g + 1) * BLOCK)
        left = jnp.concatenate(
            [
                signal_ref[b * channels + g * GROUP : b * channels + (g + 1) * GROUP, :]
                for b in range(blocks)
            ],
            axis=0,
        )
        hi, lo = halves(left)
        wide = dot_nt(jnp.concatenate([hi, lo], axis=0), into_hi[rows, :])
        size = left.shape[0]
        added = wide[:size] + wide[size:] + dot_nt(hi, into_lo[rows, :])
        fade = jnp.exp(-float(BLOCK) * decay_ref[g : g + 1, :])
        state = jnp.zeros((GROUP, BLOCK), f32)
        for b in range(blocks):
            place = g * size + b * GROUP
            states_ref[place : place + GROUP, :] = state
            state = fade * state + jnp.where(own, added[b * GROUP : (b + 1) * GROUP], 0.0)
        end = jnp.sum(state, axis=0, keepdims=True)
        for j in range(last_ref.shape[0]):
            last_ref[j, g : g + 1, :] = end


def within_kernel(signal_ref, taps_ref, result_ref):
    channels = taps_ref.shape[0]
    blocks = signal_ref.shape[0] // channels
    upper = upper_mask()

    def one(c, carry):
        ring = circulant(taps_ref[pl.ds(c, 1), :])
        hi_band, lo_band = halves(jnp.where(upper, ring, 0.0))
        hi, lo = halves(signal_ref[pl.ds(c, blocks, stride=channels), :])
        wide = dot(jnp.concatenate([hi, lo], axis=0), hi_band)
        total = wide[:blocks] + wide[blocks:] + dot(hi, lo_band)
        result_ref[pl.ds(c, blocks, stride=channels), :] = total
        return carry

    lax.fori_loop(0, channels, one, 0, unroll=UNROLL)


def finish_kernel(
    index_ref, within_ref, states_ref, last_ref, out_hi, out_lo, decay_ref,
    long_query_ref, result_ref, ys,
):
    groups = decay_ref.shape[0]
    channels = groups * GROUP
    blocks = within_ref.shape[0] // channels
    length = blocks * BLOCK
    own = own_lanes()
    place = index_ref[0]
    decay = decay_ref[...]
    carry = jnp.zeros_like(decay)
    for j in range(last_ref.shape[0]):
        gap = (place - 1 - j).astype(f32)
        faded = jnp.exp(-float(length) * jnp.maximum(gap, 0.0) * decay) * last_ref[j]
        carry = carry + jnp.where(gap >= 0.0, faded, jnp.zeros_like(faded))
    for g in range(groups):
        rows = slice(g * BLOCK, (g + 1) * BLOCK)
        fade = jnp.exp(-float(BLOCK) * decay[g : g + 1, :])
        arriving = jnp.where(own, jnp.broadcast_to(carry[g : g + 1, :], (GROUP, BLOCK)), 0.0)
        size = blocks * GROUP
        parts = []
        for b in range(blocks):
            at = g * size + b * GROUP
            parts.append(states_ref[at : at + GROUP, :] + arriving)
            arriving = arriving * fade
        hi, lo = halves(jnp.concatenate(parts, axis=0))
        wide = dot(jnp.concatenate([hi, lo], axis=0), out_hi[rows, :])
        total = wide[:size] + wide[size:] + dot(hi, out_lo[rows, :])
        for b in range(blocks):
            at = b * channels + g * GROUP
            ys[at : at + GROUP, :] = total[b * GROUP : (b + 1) * GROUP]
    for b in range(blocks):
        cols = slice(b * BLOCK, (b + 1) * BLOCK)
        rows = slice(b * channels, (b + 1) * channels)
        result_ref[:, cols] = long_query_ref[:, cols].astype(f32) * (
            ys[rows, :] + within_ref[rows, :]
        )


def sum_over_channels(squares, later):
    both = lax.psum(squares, "core")
    half = squares.shape[0] // 2
    core = lax.axis_index("core")
    mine = lax.dynamic_slice_in_dim(both, core * half, half, 0).astype(bf16)
    count = lax.axis_size("z")
    spread = jnp.broadcast_to(mine[None], (count,) + mine.shape)
    spread, later = lax.optimization_barrier((spread, later))
    gathered = lax.all_to_all(spread, "z", split_axis=0, concat_axis=0, tiled=True)
    own = jnp.sum(gathered.astype(f32), axis=0)
    zero = jnp.zeros_like(own)
    placed = jnp.concatenate(
        [jnp.where(core == 0, own, zero), jnp.where(core == 0, zero, own)]
    )
    return lax.psum(placed, "core"), later


def shape(rows, lanes, dtype=f32):
    return jax.ShapeDtypeStruct((rows, lanes), dtype)


def shards(
    short_query,
    short_key,
    short_value,
    short_taps,
    norm_gain,
    long_key,
    long_query,
    residues,
    decay_rates,
):
    channels, length = short_value.shape
    modes = residues.shape[0]
    groups = channels // GROUP
    blocks = length // BLOCK
    devices = lax.axis_size("ctx")
    rows = blocks * channels
    vmem = pl.BlockSpec(memory_space=pltpu.VMEM)
    hbm = pl.BlockSpec(memory_space=pltpu.HBM)

    short_mix, last = call(
        short_kernel,
        [shape(rows, BLOCK), shape(channels, BLOCK)],
        [hbm] * 3,
        [vmem] * 2,
        [
            pltpu.VMEM((channels, BLOCK), bf16),
            pltpu.VMEM((channels, length), bf16),
            pltpu.VMEM((channels, length), bf16),
            pltpu.VMEM((channels, BLOCK), f32),
            pltpu.VMEM((rows, BLOCK), f32),
            pltpu.VMEM((rows + channels, BLOCK), f32),
            pltpu.SemaphoreType.DMA((2 * PARTS + 1,)),
        ],
        flops=1 << 28,
        bytes_accessed=2 << 20,
        limit=None,
    )(short_taps, short_key, short_value)
    halo = lax.ppermute(last, "ctx", [(i, i + 1) for i in range(devices - 1)])
    mixed, rest, first, query, key = call(
        gate_kernel,
        [shape(rows, BLOCK), shape(blocks, BLOCK)] + [shape(channels, BLOCK)] * 3,
        [vmem] * 2 + [hbm] * 2,
        [vmem] * 5,
        [pltpu.VMEM((channels, length), bf16)] * 2 + [pltpu.SemaphoreType.DMA((2,))],
        flops=1 << 24,
        bytes_accessed=2 << 20,
    )(short_mix, norm_gain.reshape(1, channels), short_query, long_key)
    mixed_first, squares = call(
        join_kernel,
        [shape(channels, BLOCK), shape(blocks, BLOCK)],
        [vmem] * 5,
        [vmem] * 2,
    )(first, halo, query, key, rest)

    total, (residues, decay_rates) = sum_over_channels(squares, (residues, decay_rates))
    weights = residues * jnp.sqrt(-jnp.expm1(-2.0 * decay_rates))

    def columns(value):
        return (
            value.reshape(modes, groups, GROUP).transpose(0, 2, 1).reshape(modes * GROUP, groups)
        )

    decay_cols = columns(decay_rates)
    decay_rows = decay_cols.T
    into_hi, into_lo, out_hi, out_lo, long_taps = call(
        table_kernel,
        [shape(groups * BLOCK, BLOCK, bf16)] * 4 + [shape(channels, BLOCK)],
        [vmem] * 2,
        [vmem] * 5,
        flops=1 << 26,
        bytes_accessed=2 << 20,
    )(decay_cols, columns(weights))
    signal, states, ends = call(
        state_kernel,
        [
            shape(rows, BLOCK),
            shape(rows, BLOCK),
            jax.ShapeDtypeStruct((devices, groups, BLOCK), f32),
        ],
        [vmem] * 6,
        [vmem] * 3,
        bytes_accessed=2 << 20,
        flops=1 << 27,
    )(mixed_first, mixed, total, into_hi, into_lo, decay_rows)
    ends = lax.all_to_all(ends, "ctx", split_axis=0, concat_axis=0, tiled=True)
    within = call(
        within_kernel,
        shape(rows, BLOCK),
        [vmem] * 2,
        vmem,
        bytes_accessed=2 << 20,
        flops=1 << 29,
    )(signal, long_taps)
    place = lax.axis_index("ctx").astype(jnp.int32).reshape(1)
    return call(
        finish_kernel,
        shape(channels, length),
        [pl.BlockSpec(memory_space=pltpu.SMEM)] + [vmem] * 7,
        vmem,
        [pltpu.VMEM((rows, BLOCK), f32)],
        bytes_accessed=2 << 20,
        flops=1 << 27,
    )(place, within, states, ends, out_hi, out_lo, decay_rows, long_query)


def solution(mesh):
    split = Mesh(
        mesh.devices.reshape(mesh.shape["ctx"], mesh.shape["tp"] // 2, 2),
        ("ctx", "z", "core"),
    )
    in_specs = (
        P(TP, "ctx"),
        P(TP, "ctx"),
        P(TP, "ctx"),
        P(TP, None),
        P(TP),
        P(TP, "ctx"),
        P(TP, "ctx"),
        P(None, TP),
        P(None, TP),
    )
    return jax.shard_map(
        shards, mesh=split, in_specs=in_specs, out_specs=P(TP, "ctx"), check_vma=False
    )
```

```python
import jax
import jax.numpy as jnp
from jax import lax
from jax.experimental import pallas as pl
from jax.experimental.pallas import tpu as pltpu
from jax.sharding import Mesh
from jax.sharding import PartitionSpec as P

D = 4096
TP = ("z", "core")
BLOCK = 128
GROUP = 8
UNROLL = 32
PARTS = 2
INTERPRET = False
f32 = jnp.float32
bf16 = jnp.bfloat16


def call(kernel, out_shape, in_specs, out_specs, scratch=(), flops=0, bytes_accessed=0, limit=40 << 20):
    return pl.pallas_call(
        kernel,
        out_shape=out_shape,
        in_specs=in_specs,
        out_specs=out_specs,
        scratch_shapes=list(scratch),
        compiler_params=pltpu.CompilerParams(vmem_limit_bytes=limit),
        cost_estimate=pl.CostEstimate(
            flops=flops, bytes_accessed=bytes_accessed, transcendentals=0
        ),
        interpret=INTERPRET,
    )


def halves(value):
    high = value.astype(bf16)
    return high, (value - high.astype(f32)).astype(bf16)


def circulant(row):
    spread = jnp.broadcast_to(row, (BLOCK, BLOCK))
    return pltpu.roll(spread, 0, 1, stride=1, stride_axis=0)


def dot(left, right):
    return lax.dot_general(
        left, right, (((1,), (0,)), ((), ())), preferred_element_type=f32
    )


def dot_nt(left, right):
    return lax.dot_general(
        left, right, (((1,), (1,)), ((), ())), preferred_element_type=f32
    )


def upper_mask():
    row = lax.broadcasted_iota(jnp.int32, (BLOCK, BLOCK), 0)
    lane = lax.broadcasted_iota(jnp.int32, (BLOCK, BLOCK), 1)
    return lane >= row


def own_lanes():
    row = lax.broadcasted_iota(jnp.int32, (GROUP, BLOCK), 0)
    lane = lax.broadcasted_iota(jnp.int32, (GROUP, BLOCK), 1)
    return lane % GROUP == row


def short_kernel(
    taps_hbm, key_hbm, value_hbm, mixed_ref, last_ref,
    taps_ref, key_ref, value_ref, taps, xs, ps, sems,
):
    channels, length = key_ref.shape
    blocks = length // BLOCK
    part = channels // PARTS
    first = pltpu.make_async_copy(taps_hbm, taps_ref, sems.at[2 * PARTS])
    first.start()
    copies = []
    for i in range(PARTS):
        rows = pl.ds(i * part, part)
        pair = [
            pltpu.make_async_copy(source.at[rows], target.at[rows], sems.at[2 * i + k])
            for k, (source, target) in enumerate(
                ((key_hbm, key_ref), (value_hbm, value_ref))
            )
        ]
        for copy in pair:
            copy.start()
        copies.append(pair)
    upper = upper_mask()

    def one(c, carry):
        ring = circulant(taps[pl.ds(c, 1), :])
        zero = jnp.zeros_like(ring)
        band = jnp.concatenate(
            [jnp.where(upper, ring, zero), jnp.where(upper, zero, ring)], axis=1
        ).astype(bf16)
        both = dot(xs[pl.ds(c, blocks, stride=channels), :].astype(bf16), band)
        mixed_ref[pl.ds(c, blocks, stride=channels), :] = both[:, :BLOCK]
        ps[pl.ds(c + channels, blocks, stride=channels), :] = both[:, BLOCK:]
        return carry

    first.wait()
    taps[...] = taps_ref[...].astype(f32)
    for i in range(PARTS):
        for copy in copies[i]:
            copy.wait()
        own = slice(i * part, (i + 1) * part)
        for b in range(blocks):
            cols = slice(b * BLOCK, (b + 1) * BLOCK)
            at = b * channels + i * part
            xs[at : at + part, :] = key_ref[own, cols].astype(f32) * value_ref[
                own, cols
            ].astype(f32)
        lax.fori_loop(i * part, (i + 1) * part, one, 0, unroll=UNROLL)
    last_ref[...] = ps[blocks * channels :, :]
    mixed_ref[channels:, :] += ps[channels : blocks * channels, :]


def gate_kernel(
    taps_ref, gain_ref, query_hbm, key_hbm,
    mixed_ref, squares_ref, open_mix, open_query, open_key, query_ref, key_ref, sems,
):
    copies = [
        pltpu.make_async_copy(query_hbm, query_ref, sems.at[0]),
        pltpu.make_async_copy(key_hbm, key_ref, sems.at[1]),
    ]
    for copy in copies:
        copy.start()
    channels, length = query_ref.shape
    blocks = length // BLOCK
    row = lax.broadcasted_iota(jnp.int32, (channels, channels), 0)
    lane = lax.broadcasted_iota(jnp.int32, (channels, channels), 1)
    spread = jnp.broadcast_to(gain_ref[...], (channels, channels))
    gain = jnp.sum(jnp.where(row == lane, spread, 0.0), axis=1, keepdims=True)
    for copy in copies:
        copy.wait()
    open_query[...] = query_ref[:, :BLOCK].astype(f32)
    open_key[...] = gain * key_ref[:, :BLOCK].astype(f32)
    open_mix[...] = taps_ref[:channels, :]
    mixed_ref[:channels, :] = jnp.zeros((channels, BLOCK), f32)
    squares_ref[0:1, :] = jnp.zeros((1, BLOCK), f32)
    for b in range(1, blocks):
        cols = slice(b * BLOCK, (b + 1) * BLOCK)
        rows = slice(b * channels, (b + 1) * channels)
        gated = query_ref[:, cols].astype(f32) * taps_ref[rows, :]
        squares_ref[b : b + 1, :] = jnp.sum(gated * gated, axis=0, keepdims=True)
        mixed_ref[rows, :] = gated * gain * key_ref[:, cols].astype(f32)


def table_kernel(decay_ref, weight_ref, into_hi, into_lo, out_hi, out_lo, long_taps_ref):
    groups = decay_ref.shape[1]
    lane = lax.broadcasted_iota(jnp.int32, (1, BLOCK), 1).astype(f32)
    for g in range(groups):
        rows = slice(g * BLOCK, (g + 1) * BLOCK)
        decay = decay_ref[:, g : g + 1]
        weight = weight_ref[:, g : g + 1]
        into_hi[rows, :], into_lo[rows, :] = halves(jnp.exp(-decay * (BLOCK - lane)))
        out = weight * jnp.exp(-decay * lane)
        out_hi[rows, :], out_lo[rows, :] = halves(out)
        long_taps_ref[g * GROUP : (g + 1) * GROUP, :] = jnp.sum(
            out.reshape(BLOCK // GROUP, GROUP, BLOCK), axis=0
        )


def join_kernel(short_ref, halo_ref, query_ref, key_ref, rest_ref, mixed_ref, squares_ref):
    gated = query_ref[...] * (short_ref[...] + halo_ref[...])
    squares_ref[...] = rest_ref[...]
    squares_ref[0:1, :] = jnp.sum(gated * gated, axis=0, keepdims=True)
    mixed_ref[...] = gated * key_ref[...]


def state_kernel(
    first_ref, mixed_ref, squares_ref, into_hi, into_lo, decay_ref,
    signal_ref, states_ref, last_ref,
):
    groups = decay_ref.shape[0]
    channels = groups * GROUP
    blocks = mixed_ref.shape[0] // channels
    own = own_lanes()
    scales = lax.rsqrt(squares_ref[...] / D + 1e-06)
    signal_ref[:channels, :] = first_ref[...] * scales[0:1, :]
    for b in range(1, blocks):
        rows = slice(b * channels, (b + 1) * channels)
        signal_ref[rows, :] = mixed_ref[rows, :] * scales[b : b + 1, :]
    for g in range(groups):
        rows = slice(g * BLOCK, (g + 1) * BLOCK)
        left = jnp.concatenate(
            [
                signal_ref[b * channels + g * GROUP : b * channels + (g + 1) * GROUP, :]
                for b in range(blocks)
            ],
            axis=0,
        )
        hi, lo = halves(left)
        wide = dot_nt(jnp.concatenate([hi, lo], axis=0), into_hi[rows, :])
        size = left.shape[0]
        added = wide[:size] + wide[size:] + dot_nt(hi, into_lo[rows, :])
        fade = jnp.exp(-float(BLOCK) * decay_ref[g : g + 1, :])
        state = jnp.zeros((GROUP, BLOCK), f32)
        for b in range(blocks):
            place = g * size + b * GROUP
            states_ref[place : place + GROUP, :] = state
            state = fade * state + jnp.where(own, added[b * GROUP : (b + 1) * GROUP], 0.0)
        end = jnp.sum(state, axis=0, keepdims=True)
        for j in range(last_ref.shape[0]):
            last_ref[j, g : g + 1, :] = end


def within_kernel(signal_ref, taps_ref, result_ref):
    channels = taps_ref.shape[0]
    blocks = signal_ref.shape[0] // channels
    upper = upper_mask()

    def one(c, carry):
        ring = circulant(taps_ref[pl.ds(c, 1), :])
        hi_band, lo_band = halves(jnp.where(upper, ring, 0.0))
        hi, lo = halves(signal_ref[pl.ds(c, blocks, stride=channels), :])
        wide = dot(jnp.concatenate([hi, lo], axis=0), hi_band)
        total = wide[:blocks] + wide[blocks:] + dot(hi, lo_band)
        result_ref[pl.ds(c, blocks, stride=channels), :] = total
        return carry

    lax.fori_loop(0, channels, one, 0, unroll=UNROLL)


def finish_kernel(
    index_ref, within_ref, states_ref, last_ref, out_hi, out_lo, decay_ref,
    long_query_ref, result_ref, ys,
):
    groups = decay_ref.shape[0]
    channels = groups * GROUP
    blocks = within_ref.shape[0] // channels
    length = blocks * BLOCK
    own = own_lanes()
    place = index_ref[0]
    decay = decay_ref[...]
    carry = jnp.zeros_like(decay)
    for j in range(last_ref.shape[0]):
        gap = (place - 1 - j).astype(f32)
        faded = jnp.exp(-float(length) * jnp.maximum(gap, 0.0) * decay) * last_ref[j]
        carry = carry + jnp.where(gap >= 0.0, faded, jnp.zeros_like(faded))
    for g in range(groups):
        rows = slice(g * BLOCK, (g + 1) * BLOCK)
        fade = jnp.exp(-float(BLOCK) * decay[g : g + 1, :])
        arriving = jnp.where(own, jnp.broadcast_to(carry[g : g + 1, :], (GROUP, BLOCK)), 0.0)
        size = blocks * GROUP
        parts = []
        for b in range(blocks):
            at = g * size + b * GROUP
            parts.append(states_ref[at : at + GROUP, :] + arriving)
            arriving = arriving * fade
        hi, lo = halves(jnp.concatenate(parts, axis=0))
        wide = dot(jnp.concatenate([hi, lo], axis=0), out_hi[rows, :])
        total = wide[:size] + wide[size:] + dot(hi, out_lo[rows, :])
        for b in range(blocks):
            at = b * channels + g * GROUP
            ys[at : at + GROUP, :] = total[b * GROUP : (b + 1) * GROUP]
    for b in range(blocks):
        cols = slice(b * BLOCK, (b + 1) * BLOCK)
        rows = slice(b * channels, (b + 1) * channels)
        result_ref[:, cols] = long_query_ref[:, cols].astype(f32) * (
            ys[rows, :] + within_ref[rows, :]
        )


def sum_over_channels(squares, later):
    both = lax.psum(squares, "core")
    half = squares.shape[0] // 2
    core = lax.axis_index("core")
    mine = lax.dynamic_slice_in_dim(both, core * half, half, 0).astype(bf16)
    count = lax.axis_size("z")
    spread = jnp.broadcast_to(mine[None], (count,) + mine.shape)
    spread, later = lax.optimization_barrier((spread, later))
    gathered = lax.all_to_all(spread, "z", split_axis=0, concat_axis=0, tiled=True, axis_index_groups=[[(i + 16) % 32 for i in range(32)]])
    own = jnp.sum(gathered.astype(f32), axis=0)
    zero = jnp.zeros_like(own)
    placed = jnp.concatenate(
        [jnp.where(core == 0, own, zero), jnp.where(core == 0, zero, own)]
    )
    return lax.psum(placed, "core"), later


def shape(rows, lanes, dtype=f32):
    return jax.ShapeDtypeStruct((rows, lanes), dtype)


def shards(
    short_query,
    short_key,
    short_value,
    short_taps,
    norm_gain,
    long_key,
    long_query,
    residues,
    decay_rates,
):
    channels, length = short_value.shape
    modes = residues.shape[0]
    groups = channels // GROUP
    blocks = length // BLOCK
    devices = lax.axis_size("ctx")
    rows = blocks * channels
    vmem = pl.BlockSpec(memory_space=pltpu.VMEM)
    hbm = pl.BlockSpec(memory_space=pltpu.HBM)

    short_mix, last = call(
        short_kernel,
        [shape(rows, BLOCK), shape(channels, BLOCK)],
        [hbm] * 3,
        [vmem] * 2,
        [
            pltpu.VMEM((channels, BLOCK), bf16),
            pltpu.VMEM((channels, length), bf16),
            pltpu.VMEM((channels, length), bf16),
            pltpu.VMEM((channels, BLOCK), f32),
            pltpu.VMEM((rows, BLOCK), f32),
            pltpu.VMEM((rows + channels, BLOCK), f32),
            pltpu.SemaphoreType.DMA((2 * PARTS + 1,)),
        ],
        flops=1 << 28,
        bytes_accessed=2 << 20,
        limit=None,
    )(short_taps, short_key, short_value)
    halo = lax.ppermute(last, "ctx", [(i, i + 1) for i in range(devices - 1)])
    mixed, rest, first, query, key = call(
        gate_kernel,
        [shape(rows, BLOCK), shape(blocks, BLOCK)] + [shape(channels, BLOCK)] * 3,
        [vmem] * 2 + [hbm] * 2,
        [vmem] * 5,
        [pltpu.VMEM((channels, length), bf16)] * 2 + [pltpu.SemaphoreType.DMA((2,))],
        flops=1 << 24,
        bytes_accessed=2 << 20,
    )(short_mix, norm_gain.reshape(1, channels), short_query, long_key)
    mixed_first, squares = call(
        join_kernel,
        [shape(channels, BLOCK), shape(blocks, BLOCK)],
        [vmem] * 5,
        [vmem] * 2,
    )(first, halo, query, key, rest)

    total, (residues, decay_rates) = sum_over_channels(squares, (residues, decay_rates))
    weights = residues * jnp.sqrt(-jnp.expm1(-2.0 * decay_rates))

    def columns(value):
        return (
            value.reshape(modes, groups, GROUP).transpose(0, 2, 1).reshape(modes * GROUP, groups)
        )

    decay_cols = columns(decay_rates)
    decay_rows = decay_cols.T
    into_hi, into_lo, out_hi, out_lo, long_taps = call(
        table_kernel,
        [shape(groups * BLOCK, BLOCK, bf16)] * 4 + [shape(channels, BLOCK)],
        [vmem] * 2,
        [vmem] * 5,
        flops=1 << 26,
        bytes_accessed=2 << 20,
    )(decay_cols, columns(weights))
    signal, states, ends = call(
        state_kernel,
        [
            shape(rows, BLOCK),
            shape(rows, BLOCK),
            jax.ShapeDtypeStruct((devices, groups, BLOCK), f32),
        ],
        [vmem] * 6,
        [vmem] * 3,
        bytes_accessed=2 << 20,
        flops=1 << 27,
    )(mixed_first, mixed, total, into_hi, into_lo, decay_rows)
    ends = lax.all_to_all(ends, "ctx", split_axis=0, concat_axis=0, tiled=True)
    within = call(
        within_kernel,
        shape(rows, BLOCK),
        [vmem] * 2,
        vmem,
        bytes_accessed=2 << 20,
        flops=1 << 29,
    )(signal, long_taps)
    place = lax.axis_index("ctx").astype(jnp.int32).reshape(1)
    return call(
        finish_kernel,
        shape(channels, length),
        [pl.BlockSpec(memory_space=pltpu.SMEM)] + [vmem] * 7,
        vmem,
        [pltpu.VMEM((rows, BLOCK), f32)],
        bytes_accessed=2 << 20,
        flops=1 << 27,
    )(place, within, states, ends, out_hi, out_lo, decay_rows, long_query)


def solution(mesh):
    split = Mesh(
        mesh.devices.reshape(mesh.shape["ctx"], mesh.shape["tp"] // 2, 2),
        ("ctx", "z", "core"),
    )
    in_specs = (
        P(TP, "ctx"),
        P(TP, "ctx"),
        P(TP, "ctx"),
        P(TP, None),
        P(TP),
        P(TP, "ctx"),
        P(TP, "ctx"),
        P(None, TP),
        P(None, TP),
    )
    return jax.shard_map(
        shards, mesh=split, in_specs=in_specs, out_specs=P(TP, "ctx"), check_vma=False
    )
```

```python
import jax
import jax.numpy as jnp
from jax import lax
from jax.experimental import pallas as pl
from jax.experimental.pallas import tpu as pltpu
from jax.sharding import Mesh
from jax.sharding import PartitionSpec as P

D = 4096
TP = ("z", "core")
BLOCK = 128
GROUP = 8
UNROLL = 32
PARTS = 2
INTERPRET = False
f32 = jnp.float32
bf16 = jnp.bfloat16


def call(kernel, out_shape, in_specs, out_specs, scratch=(), flops=0, bytes_accessed=0, limit=40 << 20):
    return pl.pallas_call(
        kernel,
        out_shape=out_shape,
        in_specs=in_specs,
        out_specs=out_specs,
        scratch_shapes=list(scratch),
        compiler_params=pltpu.CompilerParams(vmem_limit_bytes=limit),
        cost_estimate=pl.CostEstimate(
            flops=flops, bytes_accessed=bytes_accessed, transcendentals=0
        ),
        interpret=INTERPRET,
    )


def halves(value):
    high = value.astype(bf16)
    return high, (value - high.astype(f32)).astype(bf16)


def circulant(row):
    spread = jnp.broadcast_to(row, (BLOCK, BLOCK))
    return pltpu.roll(spread, 0, 1, stride=1, stride_axis=0)


def dot(left, right):
    return lax.dot_general(
        left, right, (((1,), (0,)), ((), ())), preferred_element_type=f32
    )


def dot_nt(left, right):
    return lax.dot_general(
        left, right, (((1,), (1,)), ((), ())), preferred_element_type=f32
    )


def upper_mask():
    row = lax.broadcasted_iota(jnp.int32, (BLOCK, BLOCK), 0)
    lane = lax.broadcasted_iota(jnp.int32, (BLOCK, BLOCK), 1)
    return lane >= row


def own_lanes():
    row = lax.broadcasted_iota(jnp.int32, (GROUP, BLOCK), 0)
    lane = lax.broadcasted_iota(jnp.int32, (GROUP, BLOCK), 1)
    return lane % GROUP == row


def short_kernel(
    taps_hbm, key_hbm, value_hbm, mixed_ref, last_ref,
    taps_ref, key_ref, value_ref, taps, xs, ps, sems,
):
    channels, length = key_ref.shape
    blocks = length // BLOCK
    part = channels // PARTS
    first = pltpu.make_async_copy(taps_hbm, taps_ref, sems.at[2 * PARTS])
    first.start()
    copies = []
    for i in range(PARTS):
        rows = pl.ds(i * part, part)
        pair = [
            pltpu.make_async_copy(source.at[rows], target.at[rows], sems.at[2 * i + k])
            for k, (source, target) in enumerate(
                ((key_hbm, key_ref), (value_hbm, value_ref))
            )
        ]
        for copy in pair:
            copy.start()
        copies.append(pair)
    upper = upper_mask()

    def one(c, carry):
        ring = circulant(taps[pl.ds(c, 1), :])
        zero = jnp.zeros_like(ring)
        band = jnp.concatenate(
            [jnp.where(upper, ring, zero), jnp.where(upper, zero, ring)], axis=1
        ).astype(bf16)
        both = dot(xs[pl.ds(c, blocks, stride=channels), :].astype(bf16), band)
        mixed_ref[pl.ds(c, blocks, stride=channels), :] = both[:, :BLOCK]
        ps[pl.ds(c + channels, blocks, stride=channels), :] = both[:, BLOCK:]
        return carry

    first.wait()
    taps[...] = taps_ref[...].astype(f32)
    for i in range(PARTS):
        for copy in copies[i]:
            copy.wait()
        own = slice(i * part, (i + 1) * part)
        for b in range(blocks):
            cols = slice(b * BLOCK, (b + 1) * BLOCK)
            at = b * channels + i * part
            xs[at : at + part, :] = key_ref[own, cols].astype(f32) * value_ref[
                own, cols
            ].astype(f32)
        lax.fori_loop(i * part, (i + 1) * part, one, 0, unroll=UNROLL)
    last_ref[...] = ps[blocks * channels :, :].astype(bf16)
    mixed_ref[channels:, :] += ps[channels : blocks * channels, :]


def gate_kernel(
    taps_ref, gain_ref, query_hbm, key_hbm,
    mixed_ref, squares_ref, open_mix, open_query, open_key, query_ref, key_ref, sems,
):
    copies = [
        pltpu.make_async_copy(query_hbm, query_ref, sems.at[0]),
        pltpu.make_async_copy(key_hbm, key_ref, sems.at[1]),
    ]
    for copy in copies:
        copy.start()
    channels, length = query_ref.shape
    blocks = length // BLOCK
    row = lax.broadcasted_iota(jnp.int32, (channels, channels), 0)
    lane = lax.broadcasted_iota(jnp.int32, (channels, channels), 1)
    spread = jnp.broadcast_to(gain_ref[...], (channels, channels))
    gain = jnp.sum(jnp.where(row == lane, spread, 0.0), axis=1, keepdims=True)
    for copy in copies:
        copy.wait()
    open_query[...] = query_ref[:, :BLOCK].astype(f32)
    open_key[...] = gain * key_ref[:, :BLOCK].astype(f32)
    open_mix[...] = taps_ref[:channels, :]
    mixed_ref[:channels, :] = jnp.zeros((channels, BLOCK), f32)
    squares_ref[0:1, :] = jnp.zeros((1, BLOCK), f32)
    for b in range(1, blocks):
        cols = slice(b * BLOCK, (b + 1) * BLOCK)
        rows = slice(b * channels, (b + 1) * channels)
        gated = query_ref[:, cols].astype(f32) * taps_ref[rows, :]
        squares_ref[b : b + 1, :] = jnp.sum(gated * gated, axis=0, keepdims=True)
        mixed_ref[rows, :] = gated * gain * key_ref[:, cols].astype(f32)


def table_kernel(decay_ref, weight_ref, into_hi, into_lo, out_hi, out_lo, long_taps_ref):
    groups = decay_ref.shape[1]
    lane = lax.broadcasted_iota(jnp.int32, (1, BLOCK), 1).astype(f32)
    for g in range(groups):
        rows = slice(g * BLOCK, (g + 1) * BLOCK)
        decay = decay_ref[:, g : g + 1]
        weight = weight_ref[:, g : g + 1]
        into_hi[rows, :], into_lo[rows, :] = halves(jnp.exp(-decay * (BLOCK - lane)))
        out = weight * jnp.exp(-decay * lane)
        out_hi[rows, :], out_lo[rows, :] = halves(out)
        long_taps_ref[g * GROUP : (g + 1) * GROUP, :] = jnp.sum(
            out.reshape(BLOCK // GROUP, GROUP, BLOCK), axis=0
        )


def join_kernel(short_ref, halo_ref, query_ref, key_ref, rest_ref, mixed_ref, squares_ref):
    gated = query_ref[...] * (short_ref[...] + halo_ref[...].astype(f32))
    squares_ref[...] = rest_ref[...]
    squares_ref[0:1, :] = jnp.sum(gated * gated, axis=0, keepdims=True)
    mixed_ref[...] = gated * key_ref[...]


def state_kernel(
    first_ref, mixed_ref, squares_ref, into_hi, into_lo, decay_ref,
    signal_ref, states_ref, last_ref,
):
    groups = decay_ref.shape[0]
    channels = groups * GROUP
    blocks = mixed_ref.shape[0] // channels
    own = own_lanes()
    scales = lax.rsqrt(squares_ref[...] / D + 1e-06)
    signal_ref[:channels, :] = first_ref[...] * scales[0:1, :]
    for b in range(1, blocks):
        rows = slice(b * channels, (b + 1) * channels)
        signal_ref[rows, :] = mixed_ref[rows, :] * scales[b : b + 1, :]
    for g in range(groups):
        rows = slice(g * BLOCK, (g + 1) * BLOCK)
        left = jnp.concatenate(
            [
                signal_ref[b * channels + g * GROUP : b * channels + (g + 1) * GROUP, :]
                for b in range(blocks)
            ],
            axis=0,
        )
        hi, lo = halves(left)
        wide = dot_nt(jnp.concatenate([hi, lo], axis=0), into_hi[rows, :])
        size = left.shape[0]
        added = wide[:size] + wide[size:] + dot_nt(hi, into_lo[rows, :])
        fade = jnp.exp(-float(BLOCK) * decay_ref[g : g + 1, :])
        state = jnp.zeros((GROUP, BLOCK), f32)
        for b in range(blocks):
            place = g * size + b * GROUP
            states_ref[place : place + GROUP, :] = state
            state = fade * state + jnp.where(own, added[b * GROUP : (b + 1) * GROUP], 0.0)
        end = jnp.sum(state, axis=0, keepdims=True)
        for j in range(last_ref.shape[0]):
            last_ref[j, g : g + 1, :] = end


def within_kernel(signal_ref, taps_ref, result_ref):
    channels = taps_ref.shape[0]
    blocks = signal_ref.shape[0] // channels
    upper = upper_mask()

    def one(c, carry):
        ring = circulant(taps_ref[pl.ds(c, 1), :])
        hi_band, lo_band = halves(jnp.where(upper, ring, 0.0))
        hi, lo = halves(signal_ref[pl.ds(c, blocks, stride=channels), :])
        wide = dot(jnp.concatenate([hi, lo], axis=0), hi_band)
        total = wide[:blocks] + wide[blocks:] + dot(hi, lo_band)
        result_ref[pl.ds(c, blocks, stride=channels), :] = total
        return carry

    lax.fori_loop(0, channels, one, 0, unroll=UNROLL)


def finish_kernel(
    index_ref, within_ref, states_ref, last_ref, out_hi, out_lo, decay_ref,
    long_query_ref, result_ref, ys,
):
    groups = decay_ref.shape[0]
    channels = groups * GROUP
    blocks = within_ref.shape[0] // channels
    length = blocks * BLOCK
    own = own_lanes()
    place = index_ref[0]
    decay = decay_ref[...]
    carry = jnp.zeros_like(decay)
    devices = last_ref.shape[0]
    for j in range(devices):
        gap = (place - 1 - j).astype(f32)
        slot = (j - devices // 2) % devices
        faded = jnp.exp(-float(length) * jnp.maximum(gap, 0.0) * decay) * last_ref[slot]
        carry = carry + jnp.where(gap >= 0.0, faded, jnp.zeros_like(faded))
    for g in range(groups):
        rows = slice(g * BLOCK, (g + 1) * BLOCK)
        fade = jnp.exp(-float(BLOCK) * decay[g : g + 1, :])
        arriving = jnp.where(own, jnp.broadcast_to(carry[g : g + 1, :], (GROUP, BLOCK)), 0.0)
        size = blocks * GROUP
        parts = []
        for b in range(blocks):
            at = g * size + b * GROUP
            parts.append(states_ref[at : at + GROUP, :] + arriving)
            arriving = arriving * fade
        hi, lo = halves(jnp.concatenate(parts, axis=0))
        wide = dot(jnp.concatenate([hi, lo], axis=0), out_hi[rows, :])
        total = wide[:size] + wide[size:] + dot(hi, out_lo[rows, :])
        for b in range(blocks):
            at = b * channels + g * GROUP
            ys[at : at + GROUP, :] = total[b * GROUP : (b + 1) * GROUP]
    for b in range(blocks):
        cols = slice(b * BLOCK, (b + 1) * BLOCK)
        rows = slice(b * channels, (b + 1) * channels)
        result_ref[:, cols] = long_query_ref[:, cols].astype(f32) * (
            ys[rows, :] + within_ref[rows, :]
        )


def exchange(spread, axis, first):
    count = lax.axis_size(axis)
    group = [(first + i) % count for i in range(count)]
    return lax.all_to_all(
        spread, axis, split_axis=0, concat_axis=0, tiled=True, axis_index_groups=[group]
    )


def sum_over_channels(squares, later):
    both = lax.psum(squares, "core")
    half = squares.shape[0] // 2
    core = lax.axis_index("core")
    mine = lax.dynamic_slice_in_dim(both, core * half, half, 0).astype(bf16)
    count = lax.axis_size("z")
    spread = jnp.broadcast_to(mine[None], (count,) + mine.shape)
    spread, later = lax.optimization_barrier((spread, later))
    gathered = exchange(spread, "z", 5 * count // 8)
    own = jnp.sum(gathered.astype(f32), axis=0)
    zero = jnp.zeros_like(own)
    placed = jnp.concatenate(
        [jnp.where(core == 0, own, zero), jnp.where(core == 0, zero, own)]
    )
    return lax.psum(placed, "core"), later


def shape(rows, lanes, dtype=f32):
    return jax.ShapeDtypeStruct((rows, lanes), dtype)


def shards(
    short_query,
    short_key,
    short_value,
    short_taps,
    norm_gain,
    long_key,
    long_query,
    residues,
    decay_rates,
):
    channels, length = short_value.shape
    modes = residues.shape[0]
    groups = channels // GROUP
    blocks = length // BLOCK
    devices = lax.axis_size("ctx")
    rows = blocks * channels
    vmem = pl.BlockSpec(memory_space=pltpu.VMEM)
    hbm = pl.BlockSpec(memory_space=pltpu.HBM)

    short_mix, last = call(
        short_kernel,
        [shape(rows, BLOCK), shape(channels, BLOCK, bf16)],
        [hbm] * 3,
        [vmem] * 2,
        [
            pltpu.VMEM((channels, BLOCK), bf16),
            pltpu.VMEM((channels, length), bf16),
            pltpu.VMEM((channels, length), bf16),
            pltpu.VMEM((channels, BLOCK), f32),
            pltpu.VMEM((rows, BLOCK), f32),
            pltpu.VMEM((rows + channels, BLOCK), f32),
            pltpu.SemaphoreType.DMA((2 * PARTS + 1,)),
        ],
        flops=1 << 28,
        bytes_accessed=2 << 20,
        limit=None,
    )(short_taps, short_key, short_value)
    halo = lax.ppermute(last, "ctx", [(i, i + 1) for i in range(devices - 1)])
    mixed, rest, first, query, key = call(
        gate_kernel,
        [shape(rows, BLOCK), shape(blocks, BLOCK)] + [shape(channels, BLOCK)] * 3,
        [vmem] * 2 + [hbm] * 2,
        [vmem] * 5,
        [pltpu.VMEM((channels, length), bf16)] * 2 + [pltpu.SemaphoreType.DMA((2,))],
        flops=1 << 24,
        bytes_accessed=2 << 20,
    )(short_mix, norm_gain.reshape(1, channels), short_query, long_key)
    mixed_first, squares = call(
        join_kernel,
        [shape(channels, BLOCK), shape(blocks, BLOCK)],
        [vmem] * 5,
        [vmem] * 2,
    )(first, halo, query, key, rest)

    total, (residues, decay_rates) = sum_over_channels(squares, (residues, decay_rates))
    weights = residues * jnp.sqrt(-jnp.expm1(-2.0 * decay_rates))

    def columns(value):
        return (
            value.reshape(modes, groups, GROUP).transpose(0, 2, 1).reshape(modes * GROUP, groups)
        )

    decay_cols = columns(decay_rates)
    decay_rows = decay_cols.T
    into_hi, into_lo, out_hi, out_lo, long_taps = call(
        table_kernel,
        [shape(groups * BLOCK, BLOCK, bf16)] * 4 + [shape(channels, BLOCK)],
        [vmem] * 2,
        [vmem] * 5,
        flops=1 << 26,
        bytes_accessed=2 << 20,
    )(decay_cols, columns(weights))
    signal, states, ends = call(
        state_kernel,
        [
            shape(rows, BLOCK),
            shape(rows, BLOCK),
            jax.ShapeDtypeStruct((devices, groups, BLOCK), f32),
        ],
        [vmem] * 6,
        [vmem] * 3,
        bytes_accessed=2 << 20,
        flops=1 << 27,
    )(mixed_first, mixed, total, into_hi, into_lo, decay_rows)
    ends = exchange(ends, "ctx", devices // 2)
    within = call(
        within_kernel,
        shape(rows, BLOCK),
        [vmem] * 2,
        vmem,
        bytes_accessed=2 << 20,
        flops=1 << 29,
    )(signal, long_taps)
    place = lax.axis_index("ctx").astype(jnp.int32).reshape(1)
    return call(
        finish_kernel,
        shape(channels, length),
        [pl.BlockSpec(memory_space=pltpu.SMEM)] + [vmem] * 7,
        vmem,
        [pltpu.VMEM((rows, BLOCK), f32)],
        bytes_accessed=2 << 20,
        flops=1 << 27,
    )(place, within, states, ends, out_hi, out_lo, decay_rows, long_query)


def solution(mesh):
    split = Mesh(
        mesh.devices.reshape(mesh.shape["ctx"], mesh.shape["tp"] // 2, 2),
        ("ctx", "z", "core"),
    )
    in_specs = (
        P(TP, "ctx"),
        P(TP, "ctx"),
        P(TP, "ctx"),
        P(TP, None),
        P(TP),
        P(TP, "ctx"),
        P(TP, "ctx"),
        P(None, TP),
        P(None, TP),
    )
    return jax.shard_map(
        shards, mesh=split, in_specs=in_specs, out_specs=P(TP, "ctx"), check_vma=False
    )
```

```python
import jax
import jax.numpy as jnp
from jax import lax
from jax.experimental import pallas as pl
from jax.experimental.pallas import tpu as pltpu
from jax.sharding import Mesh
from jax.sharding import PartitionSpec as P

D = 4096
TP = ("z", "core")
BLOCK = 128
GROUP = 8
UNROLL = 32
PARTS = 2
INTERPRET = False
f32 = jnp.float32
bf16 = jnp.bfloat16


def call(kernel, out_shape, in_specs, out_specs, scratch=(), flops=0, bytes_accessed=0, limit=40 << 20):
    return pl.pallas_call(
        kernel,
        out_shape=out_shape,
        in_specs=in_specs,
        out_specs=out_specs,
        scratch_shapes=list(scratch),
        compiler_params=pltpu.CompilerParams(vmem_limit_bytes=limit),
        cost_estimate=pl.CostEstimate(
            flops=flops, bytes_accessed=bytes_accessed, transcendentals=0
        ),
        interpret=INTERPRET,
    )


def halves(value):
    high = value.astype(bf16)
    return high, (value - high.astype(f32)).astype(bf16)


def circulant(row):
    spread = jnp.broadcast_to(row, (BLOCK, BLOCK))
    return pltpu.roll(spread, 0, 1, stride=1, stride_axis=0)


def dot(left, right):
    return lax.dot_general(
        left, right, (((1,), (0,)), ((), ())), preferred_element_type=f32
    )


def dot_nt(left, right):
    return lax.dot_general(
        left, right, (((1,), (1,)), ((), ())), preferred_element_type=f32
    )


def upper_mask():
    row = lax.broadcasted_iota(jnp.int32, (BLOCK, BLOCK), 0)
    lane = lax.broadcasted_iota(jnp.int32, (BLOCK, BLOCK), 1)
    return lane >= row


def own_lanes():
    row = lax.broadcasted_iota(jnp.int32, (GROUP, BLOCK), 0)
    lane = lax.broadcasted_iota(jnp.int32, (GROUP, BLOCK), 1)
    return lane % GROUP == row


def short_kernel(
    taps_hbm, key_hbm, value_hbm, mixed_ref, last_ref,
    taps_ref, key_ref, value_ref, taps, xs, ps, sems,
):
    channels, length = key_ref.shape
    blocks = length // BLOCK
    part = channels // PARTS
    first = pltpu.make_async_copy(taps_hbm, taps_ref, sems.at[2 * PARTS])
    first.start()
    copies = []
    for i in range(PARTS):
        rows = pl.ds(i * part, part)
        pair = [
            pltpu.make_async_copy(source.at[rows], target.at[rows], sems.at[2 * i + k])
            for k, (source, target) in enumerate(
                ((key_hbm, key_ref), (value_hbm, value_ref))
            )
        ]
        for copy in pair:
            copy.start()
        copies.append(pair)
    upper = upper_mask()
    opening = lax.broadcasted_iota(jnp.int32, (blocks, BLOCK), 0) == 0

    def one(c, carry):
        ring = circulant(taps[pl.ds(c, 1), :])
        zero = jnp.zeros_like(ring)
        band = jnp.concatenate(
            [jnp.where(upper, ring, zero), jnp.where(upper, zero, ring)], axis=1
        ).astype(bf16)
        both = dot(xs[pl.ds(c, blocks, stride=channels), :].astype(bf16), band)
        behind = pltpu.roll(both[:, BLOCK:], 1, 0)
        mixed_ref[pl.ds(c * blocks, blocks), :] = both[:, :BLOCK] + jnp.where(
            opening, zero[:blocks], behind
        )
        ps[pl.ds(c, 1), :] = behind[:1]
        return carry

    first.wait()
    taps[...] = taps_ref[...].astype(f32)
    for i in range(PARTS):
        for copy in copies[i]:
            copy.wait()
        own = slice(i * part, (i + 1) * part)
        for b in range(blocks):
            cols = slice(b * BLOCK, (b + 1) * BLOCK)
            at = b * channels + i * part
            xs[at : at + part, :] = key_ref[own, cols].astype(f32) * value_ref[
                own, cols
            ].astype(f32)
        lax.fori_loop(i * part, (i + 1) * part, one, 0, unroll=UNROLL)
    last_ref[...] = ps[...].astype(bf16)


def gate_kernel(
    taps_ref, gain_ref, query_hbm, key_hbm,
    mixed_ref, squares_ref, open_mix, open_query, open_key, query_ref, key_ref, sems,
):
    copies = [
        pltpu.make_async_copy(query_hbm, query_ref, sems.at[0]),
        pltpu.make_async_copy(key_hbm, key_ref, sems.at[1]),
    ]
    for copy in copies:
        copy.start()
    channels, length = query_ref.shape
    blocks = length // BLOCK
    row = lax.broadcasted_iota(jnp.int32, (channels, channels), 0)
    lane = lax.broadcasted_iota(jnp.int32, (channels, channels), 1)
    spread = jnp.broadcast_to(gain_ref[...], (channels, channels))
    gain = jnp.sum(jnp.where(row == lane, spread, 0.0), axis=1, keepdims=True)
    for copy in copies:
        copy.wait()
    open_query[...] = query_ref[:, :BLOCK].astype(f32)
    open_key[...] = gain * key_ref[:, :BLOCK].astype(f32)
    open_mix[...] = taps_ref[pl.ds(0, channels, stride=blocks), :]
    mixed_ref[:channels, :] = jnp.zeros((channels, BLOCK), f32)
    squares_ref[0:1, :] = jnp.zeros((1, BLOCK), f32)
    for b in range(1, blocks):
        cols = slice(b * BLOCK, (b + 1) * BLOCK)
        rows = slice(b * channels, (b + 1) * channels)
        gated = query_ref[:, cols].astype(f32) * taps_ref[
            pl.ds(b, channels, stride=blocks), :
        ]
        squares_ref[b : b + 1, :] = jnp.sum(gated * gated, axis=0, keepdims=True)
        mixed_ref[rows, :] = gated * gain * key_ref[:, cols].astype(f32)


def table_kernel(decay_ref, weight_ref, into_hi, into_lo, out_hi, out_lo, long_taps_ref):
    groups = decay_ref.shape[1]
    lane = lax.broadcasted_iota(jnp.int32, (1, BLOCK), 1).astype(f32)
    for g in range(groups):
        rows = slice(g * BLOCK, (g + 1) * BLOCK)
        decay = decay_ref[:, g : g + 1]
        weight = weight_ref[:, g : g + 1]
        into_hi[rows, :], into_lo[rows, :] = halves(jnp.exp(-decay * (BLOCK - lane)))
        out = weight * jnp.exp(-decay * lane)
        out_hi[rows, :], out_lo[rows, :] = halves(out)
        long_taps_ref[g * GROUP : (g + 1) * GROUP, :] = jnp.sum(
            out.reshape(BLOCK // GROUP, GROUP, BLOCK), axis=0
        )


def join_kernel(short_ref, halo_ref, query_ref, key_ref, rest_ref, mixed_ref, squares_ref):
    gated = query_ref[...] * (short_ref[...] + halo_ref[...].astype(f32))
    squares_ref[...] = rest_ref[...]
    squares_ref[0:1, :] = jnp.sum(gated * gated, axis=0, keepdims=True)
    mixed_ref[...] = gated * key_ref[...]


def state_kernel(
    first_ref, mixed_ref, squares_ref, into_hi, into_lo, decay_ref,
    signal_ref, states_ref, last_ref,
):
    groups = decay_ref.shape[0]
    channels = groups * GROUP
    blocks = mixed_ref.shape[0] // channels
    own = own_lanes()
    scales = lax.rsqrt(squares_ref[...] / D + 1e-06)
    signal_ref[:channels, :] = first_ref[...] * scales[0:1, :]
    for b in range(1, blocks):
        rows = slice(b * channels, (b + 1) * channels)
        signal_ref[rows, :] = mixed_ref[rows, :] * scales[b : b + 1, :]
    for g in range(groups):
        rows = slice(g * BLOCK, (g + 1) * BLOCK)
        left = jnp.concatenate(
            [
                signal_ref[b * channels + g * GROUP : b * channels + (g + 1) * GROUP, :]
                for b in range(blocks)
            ],
            axis=0,
        )
        hi, lo = halves(left)
        wide = dot_nt(jnp.concatenate([hi, lo], axis=0), into_hi[rows, :])
        size = left.shape[0]
        added = wide[:size] + wide[size:] + dot_nt(hi, into_lo[rows, :])
        fade = jnp.exp(-float(BLOCK) * decay_ref[g : g + 1, :])
        state = jnp.zeros((GROUP, BLOCK), f32)
        for b in range(blocks):
            place = g * size + b * GROUP
            states_ref[place : place + GROUP, :] = state
            state = fade * state + jnp.where(own, added[b * GROUP : (b + 1) * GROUP], 0.0)
        end = jnp.sum(state, axis=0, keepdims=True)
        for j in range(last_ref.shape[0]):
            last_ref[j, g : g + 1, :] = end


def within_kernel(signal_ref, taps_ref, result_ref):
    channels = taps_ref.shape[0]
    blocks = signal_ref.shape[0] // channels
    upper = upper_mask()

    def one(c, carry):
        ring = circulant(taps_ref[pl.ds(c, 1), :])
        hi_band, lo_band = halves(jnp.where(upper, ring, 0.0))
        hi, lo = halves(signal_ref[pl.ds(c, blocks, stride=channels), :])
        wide = dot(jnp.concatenate([hi, lo], axis=0), hi_band)
        total = wide[:blocks] + wide[blocks:] + dot(hi, lo_band)
        result_ref[pl.ds(c, blocks, stride=channels), :] = total
        return carry

    lax.fori_loop(0, channels, one, 0, unroll=UNROLL)


def finish_kernel(
    index_ref, within_ref, states_ref, last_ref, out_hi, out_lo, decay_ref,
    long_query_ref, result_hbm, result_ref, sems,
):
    groups = decay_ref.shape[0]
    channels = groups * GROUP
    blocks = within_ref.shape[0] // channels
    length = blocks * BLOCK
    own = own_lanes()
    place = index_ref[0]
    decay = decay_ref[...]
    carry = jnp.zeros_like(decay)
    devices = last_ref.shape[0]
    for j in range(devices):
        gap = (place - 1 - j).astype(f32)
        slot = (j - devices // 2) % devices
        faded = jnp.exp(-float(length) * jnp.maximum(gap, 0.0) * decay) * last_ref[slot]
        carry = carry + jnp.where(gap >= 0.0, faded, jnp.zeros_like(faded))
    sends = []
    for g in range(groups):
        rows = slice(g * BLOCK, (g + 1) * BLOCK)
        fade = jnp.exp(-float(BLOCK) * decay[g : g + 1, :])
        arriving = jnp.where(own, jnp.broadcast_to(carry[g : g + 1, :], (GROUP, BLOCK)), 0.0)
        size = blocks * GROUP
        parts = []
        for b in range(blocks):
            at = g * size + b * GROUP
            parts.append(states_ref[at : at + GROUP, :] + arriving)
            arriving = arriving * fade
        hi, lo = halves(jnp.concatenate(parts, axis=0))
        wide = dot(jnp.concatenate([hi, lo], axis=0), out_hi[rows, :])
        total = wide[:size] + wide[size:] + dot(hi, out_lo[rows, :])
        strip = slice(g * GROUP, (g + 1) * GROUP)
        for b in range(blocks):
            at = b * channels + g * GROUP
            cols = slice(b * BLOCK, (b + 1) * BLOCK)
            result_ref[strip, cols] = long_query_ref[strip, cols].astype(f32) * (
                total[b * GROUP : (b + 1) * GROUP] + within_ref[at : at + GROUP, :]
            )
        send = pltpu.make_async_copy(
            result_ref.at[pl.ds(g * GROUP, GROUP)],
            result_hbm.at[pl.ds(g * GROUP, GROUP)],
            sems.at[g],
        )
        send.start()
        sends.append(send)
    for send in sends:
        send.wait()


def exchange(spread, axis, first):
    count = lax.axis_size(axis)
    group = [(first + i) % count for i in range(count)]
    return lax.all_to_all(
        spread, axis, split_axis=0, concat_axis=0, tiled=True, axis_index_groups=[group]
    )


def sum_over_channels(squares, later):
    both = lax.psum(squares, "core")
    half = squares.shape[0] // 2
    core = lax.axis_index("core")
    mine = lax.dynamic_slice_in_dim(both, core * half, half, 0).astype(bf16)
    count = lax.axis_size("z")
    spread = jnp.broadcast_to(mine[None], (count,) + mine.shape)
    spread, later = lax.optimization_barrier((spread, later))
    gathered = exchange(spread, "z", 5 * count // 8)
    own = jnp.sum(gathered.astype(f32), axis=0)
    zero = jnp.zeros_like(own)
    placed = jnp.concatenate(
        [jnp.where(core == 0, own, zero), jnp.where(core == 0, zero, own)]
    )
    return lax.psum(placed, "core"), later


def shape(rows, lanes, dtype=f32):
    return jax.ShapeDtypeStruct((rows, lanes), dtype)


def shards(
    short_query,
    short_key,
    short_value,
    short_taps,
    norm_gain,
    long_key,
    long_query,
    residues,
    decay_rates,
):
    channels, length = short_value.shape
    modes = residues.shape[0]
    groups = channels // GROUP
    blocks = length // BLOCK
    devices = lax.axis_size("ctx")
    rows = blocks * channels
    vmem = pl.BlockSpec(memory_space=pltpu.VMEM)
    hbm = pl.BlockSpec(memory_space=pltpu.HBM)

    short_mix, last = call(
        short_kernel,
        [shape(rows, BLOCK), shape(channels, BLOCK, bf16)],
        [hbm] * 3,
        [vmem] * 2,
        [
            pltpu.VMEM((channels, BLOCK), bf16),
            pltpu.VMEM((channels, length), bf16),
            pltpu.VMEM((channels, length), bf16),
            pltpu.VMEM((channels, BLOCK), f32),
            pltpu.VMEM((rows, BLOCK), f32),
            pltpu.VMEM((channels, BLOCK), f32),
            pltpu.SemaphoreType.DMA((2 * PARTS + 1,)),
        ],
        flops=1 << 28,
        bytes_accessed=2 << 20,
        limit=None,
    )(short_taps, short_key, short_value)
    halo = lax.ppermute(last, "ctx", [(i, i + 1) for i in range(devices - 1)])
    mixed, rest, first, query, key = call(
        gate_kernel,
        [shape(rows, BLOCK), shape(blocks, BLOCK)] + [shape(channels, BLOCK)] * 3,
        [vmem] * 2 + [hbm] * 2,
        [vmem] * 5,
        [pltpu.VMEM((channels, length), bf16)] * 2 + [pltpu.SemaphoreType.DMA((2,))],
        flops=1 << 24,
        bytes_accessed=2 << 20,
    )(short_mix, norm_gain.reshape(1, channels), short_query, long_key)
    mixed_first, squares = call(
        join_kernel,
        [shape(channels, BLOCK), shape(blocks, BLOCK)],
        [vmem] * 5,
        [vmem] * 2,
    )(first, halo, query, key, rest)

    total, (residues, decay_rates) = sum_over_channels(squares, (residues, decay_rates))
    weights = residues * jnp.sqrt(-jnp.expm1(-2.0 * decay_rates))

    def columns(value):
        return (
            value.reshape(modes, groups, GROUP).transpose(0, 2, 1).reshape(modes * GROUP, groups)
        )

    decay_cols = columns(decay_rates)
    decay_rows = decay_cols.T
    into_hi, into_lo, out_hi, out_lo, long_taps = call(
        table_kernel,
        [shape(groups * BLOCK, BLOCK, bf16)] * 4 + [shape(channels, BLOCK)],
        [vmem] * 2,
        [vmem] * 5,
        flops=1 << 26,
        bytes_accessed=2 << 20,
    )(decay_cols, columns(weights))
    signal, states, ends = call(
        state_kernel,
        [
            shape(rows, BLOCK),
            shape(rows, BLOCK),
            jax.ShapeDtypeStruct((devices, groups, BLOCK), f32),
        ],
        [vmem] * 6,
        [vmem] * 3,
        bytes_accessed=2 << 20,
        flops=1 << 27,
    )(mixed_first, mixed, total, into_hi, into_lo, decay_rows)
    ends = exchange(ends, "ctx", devices // 2)
    within = call(
        within_kernel,
        shape(rows, BLOCK),
        [vmem] * 2,
        vmem,
        bytes_accessed=2 << 20,
        flops=1 << 29,
    )(signal, long_taps)
    place = lax.axis_index("ctx").astype(jnp.int32).reshape(1)
    return call(
        finish_kernel,
        shape(channels, length),
        [pl.BlockSpec(memory_space=pltpu.SMEM)] + [vmem] * 7,
        hbm,
        [pltpu.VMEM((channels, length), f32), pltpu.SemaphoreType.DMA((groups,))],
        bytes_accessed=2 << 20,
        flops=1 << 27,
    )(place, within, states, ends, out_hi, out_lo, decay_rows, long_query)


def solution(mesh):
    split = Mesh(
        mesh.devices.reshape(mesh.shape["ctx"], mesh.shape["tp"] // 2, 2),
        ("ctx", "z", "core"),
    )
    in_specs = (
        P(TP, "ctx"),
        P(TP, "ctx"),
        P(TP, "ctx"),
        P(TP, None),
        P(TP),
        P(TP, "ctx"),
        P(TP, "ctx"),
        P(None, TP),
        P(None, TP),
    )
    return jax.shard_map(
        shards, mesh=split, in_specs=in_specs, out_specs=P(TP, "ctx"), check_vma=False
    )
```

```python
import jax
import jax.numpy as jnp
from jax import lax
from jax.experimental import pallas as pl
from jax.experimental.pallas import tpu as pltpu
from jax.sharding import Mesh
from jax.sharding import PartitionSpec as P

D = 4096
TP = ("z", "core")
BLOCK = 128
GROUP = 8
UNROLL = 32
PARTS = 2
INTERPRET = False
f32 = jnp.float32
bf16 = jnp.bfloat16


def call(kernel, out_shape, in_specs, out_specs, scratch=(), flops=0, bytes_accessed=0, limit=40 << 20):
    return pl.pallas_call(
        kernel,
        out_shape=out_shape,
        in_specs=in_specs,
        out_specs=out_specs,
        scratch_shapes=list(scratch),
        compiler_params=pltpu.CompilerParams(vmem_limit_bytes=limit),
        cost_estimate=pl.CostEstimate(
            flops=flops, bytes_accessed=bytes_accessed, transcendentals=0
        ),
        interpret=INTERPRET,
    )


def halves(value):
    high = value.astype(bf16)
    return high, (value - high.astype(f32)).astype(bf16)


def circulant(row):
    spread = jnp.broadcast_to(row, (BLOCK, BLOCK))
    return pltpu.roll(spread, 0, 1, stride=1, stride_axis=0)


def dot(left, right):
    return lax.dot_general(
        left, right, (((1,), (0,)), ((), ())), preferred_element_type=f32
    )


def dot_nt(left, right):
    return lax.dot_general(
        left, right, (((1,), (1,)), ((), ())), preferred_element_type=f32
    )


def upper_mask():
    row = lax.broadcasted_iota(jnp.int32, (BLOCK, BLOCK), 0)
    lane = lax.broadcasted_iota(jnp.int32, (BLOCK, BLOCK), 1)
    return lane >= row


def own_lanes():
    row = lax.broadcasted_iota(jnp.int32, (GROUP, BLOCK), 0)
    lane = lax.broadcasted_iota(jnp.int32, (GROUP, BLOCK), 1)
    return lane % GROUP == row


def short_kernel(
    taps_hbm, key_hbm, value_hbm, mixed_ref, last_ref,
    taps_ref, key_ref, value_ref, taps, xs, ps, sems,
):
    channels, length = key_ref.shape
    blocks = length // BLOCK
    part = channels // PARTS
    first = pltpu.make_async_copy(taps_hbm, taps_ref, sems.at[2 * PARTS])
    first.start()
    copies = []
    for i in range(PARTS):
        rows = pl.ds(i * part, part)
        pair = [
            pltpu.make_async_copy(source.at[rows], target.at[rows], sems.at[2 * i + k])
            for k, (source, target) in enumerate(
                ((key_hbm, key_ref), (value_hbm, value_ref))
            )
        ]
        for copy in pair:
            copy.start()
        copies.append(pair)
    upper = upper_mask()
    opening = lax.broadcasted_iota(jnp.int32, (blocks, BLOCK), 0) == 0

    def one(c, carry):
        ring = circulant(taps[pl.ds(c, 1), :])
        zero = jnp.zeros_like(ring)
        band = jnp.concatenate(
            [jnp.where(upper, ring, zero), jnp.where(upper, zero, ring)], axis=1
        ).astype(bf16)
        both = dot(xs[pl.ds(c, blocks, stride=channels), :].astype(bf16), band)
        behind = pltpu.roll(both[:, BLOCK:], 1, 0)
        mixed_ref[pl.ds(c * blocks, blocks), :] = both[:, :BLOCK] + jnp.where(
            opening, zero[:blocks], behind
        )
        ps[pl.ds(c, 1), :] = behind[:1]
        return carry

    first.wait()
    taps[...] = taps_ref[...].astype(f32)
    for i in range(PARTS):
        for copy in copies[i]:
            copy.wait()
        own = slice(i * part, (i + 1) * part)
        for b in range(blocks):
            cols = slice(b * BLOCK, (b + 1) * BLOCK)
            at = b * channels + i * part
            xs[at : at + part, :] = key_ref[own, cols].astype(f32) * value_ref[
                own, cols
            ].astype(f32)
        lax.fori_loop(i * part, (i + 1) * part, one, 0, unroll=UNROLL)
    last_ref[...] = ps[...].astype(bf16)


def gate_kernel(
    taps_ref, gain_ref, query_hbm, key_hbm,
    mixed_ref, squares_ref, open_mix, open_query, open_key, query_ref, key_ref, sems,
):
    copies = [
        pltpu.make_async_copy(query_hbm, query_ref, sems.at[0]),
        pltpu.make_async_copy(key_hbm, key_ref, sems.at[1]),
    ]
    for copy in copies:
        copy.start()
    channels, length = query_ref.shape
    blocks = length // BLOCK
    row = lax.broadcasted_iota(jnp.int32, (channels, channels), 0)
    lane = lax.broadcasted_iota(jnp.int32, (channels, channels), 1)
    spread = jnp.broadcast_to(gain_ref[...], (channels, channels))
    gain = jnp.sum(jnp.where(row == lane, spread, 0.0), axis=1, keepdims=True)
    for copy in copies:
        copy.wait()
    open_query[...] = query_ref[:, :BLOCK].astype(f32)
    open_key[...] = gain * key_ref[:, :BLOCK].astype(f32)
    open_mix[...] = taps_ref[pl.ds(0, channels, stride=blocks), :]
    mixed_ref[:channels, :] = jnp.zeros((channels, BLOCK), f32)
    squares_ref[0:1, :] = jnp.zeros((1, BLOCK), f32)
    for b in range(1, blocks):
        cols = slice(b * BLOCK, (b + 1) * BLOCK)
        rows = slice(b * channels, (b + 1) * channels)
        gated = query_ref[:, cols].astype(f32) * taps_ref[
            pl.ds(b, channels, stride=blocks), :
        ]
        squares_ref[b : b + 1, :] = jnp.sum(gated * gated, axis=0, keepdims=True)
        mixed_ref[rows, :] = gated * gain * key_ref[:, cols].astype(f32)


def table_kernel(decay_ref, weight_ref, into_hi, into_lo, out_hi, out_lo, long_taps_ref):
    groups = decay_ref.shape[1]
    lane = lax.broadcasted_iota(jnp.int32, (1, BLOCK), 1).astype(f32)
    for g in range(groups):
        rows = slice(g * BLOCK, (g + 1) * BLOCK)
        decay = decay_ref[:, g : g + 1]
        weight = weight_ref[:, g : g + 1]
        into_hi[rows, :], into_lo[rows, :] = halves(jnp.exp(-decay * (BLOCK - lane)))
        out = weight * jnp.exp(-decay * lane)
        out_hi[rows, :], out_lo[rows, :] = halves(out)
        long_taps_ref[g * GROUP : (g + 1) * GROUP, :] = jnp.sum(
            out.reshape(BLOCK // GROUP, GROUP, BLOCK), axis=0
        )


def join_kernel(short_ref, halo_ref, query_ref, key_ref, rest_ref, mixed_ref, squares_ref):
    gated = query_ref[...] * (short_ref[...] + halo_ref[...].astype(f32))
    squares_ref[...] = rest_ref[...]
    squares_ref[0:1, :] = jnp.sum(gated * gated, axis=0, keepdims=True)
    mixed_ref[...] = gated * key_ref[...]


def state_kernel(
    first_ref, mixed_ref, squares_ref, into_hi, into_lo, decay_ref,
    signal_ref, states_ref, last_ref,
):
    groups = decay_ref.shape[0]
    channels = groups * GROUP
    blocks = mixed_ref.shape[0] // channels
    own = own_lanes()
    scales = lax.rsqrt(squares_ref[...] / D + 1e-06)
    signal_ref[:channels, :] = first_ref[...] * scales[0:1, :]
    for b in range(1, blocks):
        rows = slice(b * channels, (b + 1) * channels)
        signal_ref[rows, :] = mixed_ref[rows, :] * scales[b : b + 1, :]
    for g in range(groups):
        rows = slice(g * BLOCK, (g + 1) * BLOCK)
        left = jnp.concatenate(
            [
                signal_ref[b * channels + g * GROUP : b * channels + (g + 1) * GROUP, :]
                for b in range(blocks)
            ],
            axis=0,
        )
        hi, lo = halves(left)
        wide = dot_nt(jnp.concatenate([hi, lo], axis=0), into_hi[rows, :])
        size = left.shape[0]
        added = wide[:size] + wide[size:] + dot_nt(hi, into_lo[rows, :])
        fade = jnp.exp(-float(BLOCK) * decay_ref[g : g + 1, :])
        state = jnp.zeros((GROUP, BLOCK), f32)
        for b in range(blocks):
            place = g * size + b * GROUP
            states_ref[place : place + GROUP, :] = state
            state = fade * state + jnp.where(own, added[b * GROUP : (b + 1) * GROUP], 0.0)
        end = jnp.sum(state, axis=0, keepdims=True)
        for j in range(last_ref.shape[0]):
            last_ref[j, g : g + 1, :] = end


def within_kernel(signal_ref, taps_ref, result_ref):
    channels = taps_ref.shape[0]
    blocks = signal_ref.shape[0] // channels
    upper = upper_mask()

    def one(c, carry):
        ring = circulant(taps_ref[pl.ds(c, 1), :])
        hi_band, lo_band = halves(jnp.where(upper, ring, 0.0))
        hi, lo = halves(signal_ref[pl.ds(c, blocks, stride=channels), :])
        wide = dot(jnp.concatenate([hi, lo], axis=0), hi_band)
        total = wide[:blocks] + wide[blocks:] + dot(hi, lo_band)
        result_ref[pl.ds(c, blocks, stride=channels), :] = total
        return carry

    lax.fori_loop(0, channels, one, 0, unroll=UNROLL)


def finish_kernel(
    index_ref, within_ref, states_ref, last_ref, out_hi, out_lo, decay_ref,
    long_query_ref, result_hbm, result_ref, sems,
):
    groups = decay_ref.shape[0]
    channels = groups * GROUP
    blocks = within_ref.shape[0] // channels
    length = blocks * BLOCK
    own = own_lanes()
    place = index_ref[0]
    decay = decay_ref[...]
    carry = jnp.zeros_like(decay)
    devices = last_ref.shape[0]
    for j in range(devices):
        gap = (place - 1 - j).astype(f32)
        slot = (j - devices // 2) % devices
        faded = jnp.exp(-float(length) * jnp.maximum(gap, 0.0) * decay) * last_ref[slot]
        carry = carry + jnp.where(gap >= 0.0, faded, jnp.zeros_like(faded))
    sends = []
    for g in range(groups):
        rows = slice(g * BLOCK, (g + 1) * BLOCK)
        fade = jnp.exp(-float(BLOCK) * decay[g : g + 1, :])
        arriving = jnp.where(own, jnp.broadcast_to(carry[g : g + 1, :], (GROUP, BLOCK)), 0.0)
        size = blocks * GROUP
        parts = []
        for b in range(blocks):
            at = g * size + b * GROUP
            parts.append(states_ref[at : at + GROUP, :] + arriving)
            arriving = arriving * fade
        hi, lo = halves(jnp.concatenate(parts, axis=0))
        wide = dot(jnp.concatenate([hi, lo], axis=0), out_hi[rows, :])
        total = wide[:size] + wide[size:] + dot(hi, out_lo[rows, :])
        strip = slice(g * GROUP, (g + 1) * GROUP)
        for b in range(blocks):
            at = b * channels + g * GROUP
            cols = slice(b * BLOCK, (b + 1) * BLOCK)
            result_ref[strip, cols] = long_query_ref[strip, cols].astype(f32) * (
                total[b * GROUP : (b + 1) * GROUP] + within_ref[at : at + GROUP, :]
            )
        send = pltpu.make_async_copy(
            result_ref.at[pl.ds(g * GROUP, GROUP)],
            result_hbm.at[pl.ds(g * GROUP, GROUP)],
            sems.at[g],
        )
        send.start()
        sends.append(send)
    for send in sends:
        send.wait()


def exchange(spread, axis, group):
    return lax.all_to_all(
        spread, axis, split_axis=0, concat_axis=0, tiled=True, axis_index_groups=[group]
    )


def sum_over_channels(squares, later):
    both = lax.psum(squares, "core")
    half = squares.shape[0] // 2
    core = lax.axis_index("core")
    mine = lax.dynamic_slice_in_dim(both, core * half, half, 0).astype(bf16)
    count = lax.axis_size("z")
    spread = jnp.broadcast_to(mine[None], (count,) + mine.shape)
    spread, later = lax.optimization_barrier((spread, later))
    meet, near = 5 * count // 8, count // 8
    group = [meet, *range(near), *range(meet + 1, count), *range(near, meet)]
    gathered = exchange(spread, "z", group)
    own = jnp.sum(gathered.astype(f32), axis=0)
    zero = jnp.zeros_like(own)
    placed = jnp.concatenate(
        [jnp.where(core == 0, own, zero), jnp.where(core == 0, zero, own)]
    )
    return lax.psum(placed, "core"), later


def shape(rows, lanes, dtype=f32):
    return jax.ShapeDtypeStruct((rows, lanes), dtype)


def shards(
    short_query,
    short_key,
    short_value,
    short_taps,
    norm_gain,
    long_key,
    long_query,
    residues,
    decay_rates,
):
    channels, length = short_value.shape
    modes = residues.shape[0]
    groups = channels // GROUP
    blocks = length // BLOCK
    devices = lax.axis_size("ctx")
    rows = blocks * channels
    vmem = pl.BlockSpec(memory_space=pltpu.VMEM)
    hbm = pl.BlockSpec(memory_space=pltpu.HBM)

    short_mix, last = call(
        short_kernel,
        [shape(rows, BLOCK), shape(channels, BLOCK, bf16)],
        [hbm] * 3,
        [vmem] * 2,
        [
            pltpu.VMEM((channels, BLOCK), bf16),
            pltpu.VMEM((channels, length), bf16),
            pltpu.VMEM((channels, length), bf16),
            pltpu.VMEM((channels, BLOCK), f32),
            pltpu.VMEM((rows, BLOCK), f32),
            pltpu.VMEM((channels, BLOCK), f32),
            pltpu.SemaphoreType.DMA((2 * PARTS + 1,)),
        ],
        flops=1 << 28,
        bytes_accessed=2 << 20,
        limit=None,
    )(short_taps, short_key, short_value)
    halo = lax.ppermute(last, "ctx", [(i, i + 1) for i in range(devices - 1)])
    mixed, rest, first, query, key = call(
        gate_kernel,
        [shape(rows, BLOCK), shape(blocks, BLOCK)] + [shape(channels, BLOCK)] * 3,
        [vmem] * 2 + [hbm] * 2,
        [vmem] * 5,
        [pltpu.VMEM((channels, length), bf16)] * 2 + [pltpu.SemaphoreType.DMA((2,))],
        flops=1 << 24,
        bytes_accessed=2 << 20,
    )(short_mix, norm_gain.reshape(1, channels), short_query, long_key)
    mixed_first, squares = call(
        join_kernel,
        [shape(channels, BLOCK), shape(blocks, BLOCK)],
        [vmem] * 5,
        [vmem] * 2,
    )(first, halo, query, key, rest)

    total, (residues, decay_rates) = sum_over_channels(squares, (residues, decay_rates))
    weights = residues * jnp.sqrt(-jnp.expm1(-2.0 * decay_rates))

    def columns(value):
        return (
            value.reshape(modes, groups, GROUP).transpose(0, 2, 1).reshape(modes * GROUP, groups)
        )

    decay_cols = columns(decay_rates)
    decay_rows = decay_cols.T
    into_hi, into_lo, out_hi, out_lo, long_taps = call(
        table_kernel,
        [shape(groups * BLOCK, BLOCK, bf16)] * 4 + [shape(channels, BLOCK)],
        [vmem] * 2,
        [vmem] * 5,
        flops=1 << 26,
        bytes_accessed=2 << 20,
    )(decay_cols, columns(weights))
    signal, states, ends = call(
        state_kernel,
        [
            shape(rows, BLOCK),
            shape(rows, BLOCK),
            jax.ShapeDtypeStruct((devices, groups, BLOCK), f32),
        ],
        [vmem] * 6,
        [vmem] * 3,
        bytes_accessed=2 << 20,
        flops=1 << 27,
    )(mixed_first, mixed, total, into_hi, into_lo, decay_rows)
    ends = exchange(
        ends, "ctx", [(devices // 2 + i) % devices for i in range(devices)]
    )
    within = call(
        within_kernel,
        shape(rows, BLOCK),
        [vmem] * 2,
        vmem,
        bytes_accessed=2 << 20,
        flops=1 << 29,
    )(signal, long_taps)
    place = lax.axis_index("ctx").astype(jnp.int32).reshape(1)
    return call(
        finish_kernel,
        shape(channels, length),
        [pl.BlockSpec(memory_space=pltpu.SMEM)] + [vmem] * 7,
        hbm,
        [pltpu.VMEM((channels, length), f32), pltpu.SemaphoreType.DMA((groups,))],
        bytes_accessed=2 << 20,
        flops=1 << 27,
    )(place, within, states, ends, out_hi, out_lo, decay_rows, long_query)


def solution(mesh):
    split = Mesh(
        mesh.devices.reshape(mesh.shape["ctx"], mesh.shape["tp"] // 2, 2),
        ("ctx", "z", "core"),
    )
    in_specs = (
        P(TP, "ctx"),
        P(TP, "ctx"),
        P(TP, "ctx"),
        P(TP, None),
        P(TP),
        P(TP, "ctx"),
        P(TP, "ctx"),
        P(None, TP),
        P(None, TP),
    )
    return jax.shard_map(
        shards, mesh=split, in_specs=in_specs, out_specs=P(TP, "ctx"), check_vma=False
    )
```
